1024 devices in a mesh: inpair: 32 (over y, z_hi, core), outpair: 32 (over z_lo, x).
Axes of the slice: x: 4, y: 4, z: 32 (z_hi: 4, z_lo: 8; z = z_hi * 8 + z_lo), core: 2. Of those that a mesh axis runs over, the one named last changes fastest.
Arguments:
- integrals: bfloat16 [32768, 32768], P('inpair', 'outpair'), may hold values from -0.03125 to 0.03125
- amplitudes: bfloat16 [32, 512, 32768], P('outpair', None, 'inpair'), may hold values from -6 to 6
- tile_live: int32 [128, 128], P('inpair', 'outpair'), may hold values 0 or 1
- batch_owner: int32 [2], replicated, may hold values from 0 to 31
- occ_energy: float32 [2, 512], P(None, 'inpair'), may hold values from -2 to -0.5
- vir_energy: float32 [32768], P('outpair'), may hold values from 0.5 to 4
- swap_within: int32 [32], replicated, may hold values from 0 to 31, each once
Outputs:
- update: float32 [2, 512, 32768], P(None, 'inpair', 'outpair')
The draws below stay inside these ranges and needn't reach their ends.
Inputs may be any that keep to these rules, and one draw needn't show every extreme that they name: `swap_within`: each value once.
All inputs are finite; a program needn't handle non-finite values. No bound on the sum of `tile_live` on one device may be relied on, other than what follows from the above.
Results may differ from the reference program's by a relative error of at most 0.0003.
Values may be sent and summed in bfloat16 or wider, within the bound.
A program may use at most 32 MiB of HBM per device.

```python
import jax
import jax.numpy as jnp
from jax import lax

PAIR_IN = 1024
COLS_DEV = 1024
SUB_R = 256
SUB_C = 256
ROWS = 512
NB = 2
NCD = 32768
NAB = 32768
GRP = 32
N_INPAIR = 32
N_OUTPAIR = 32


def plant(values, key, smallest, high):
    shape = values.shape
    place = [jax.random.randint(jax.random.fold_in(key, axis), (), 0, shape[axis]) for axis in range(len(shape))]
    values = values.at[tuple(place)].set(smallest)
    longest = shape.index(max(shape))
    place[longest] = (place[longest] + 1) % shape[longest]
    return values.at[tuple(place)].set(high)


def with_spikes(array, stream_key, source, target, parts, factor):
    def block_of(axis_at):
        return (jnp.arange(array.shape[axis_at]) // (array.shape[axis_at] // parts)).reshape((-1,) + (1,) * (array.ndim - 1 - axis_at))

    first = jax.random.permutation(stream_key, parts)[block_of(target)]
    far = (block_of(target) + parts // 2) % parts
    return jnp.where((block_of(source) == first) | (block_of(source) == far), factor * array, array)


def block_levels(stream_key, shape, split, smallest, top_value):
    level = 1.0
    for dim, blocks in split:
        steps = jax.random.uniform(jax.random.fold_in(jax.random.fold_in(stream_key, 6), dim), (blocks,), jnp.float32, smallest / len(split), top_value / len(split))
        level = level * jnp.repeat(jnp.exp(steps), shape[dim] // blocks).reshape((-1,) + (1,) * (len(shape) - 1 - dim))
    return level


def centred(stream_key, dims, deviation, bound, split=(), held_as=jnp.bfloat16):
    loudness = block_levels(stream_key, dims, split, -0.22, 0.18) if split else 1.0
    values = jax.random.normal(stream_key, dims, jnp.float32) * deviation * loudness
    return jnp.minimum(jnp.maximum(values, -bound), bound).astype(held_as)


def heavy_noise(key, dims, spread, most, split, heavy, kind=jnp.bfloat16):
    result = spread * jax.random.normal(key, dims, jnp.float32)
    if split:
        result = result * block_levels(key, dims, split, -0.22, 0.18)
    return jnp.clip(with_spikes(result, jax.random.fold_in(key, 3), *heavy), -most, most).astype(kind)


def setup_inputs(seed: int = 0) -> dict:
    arg_keys = jax.random.split(jax.random.key(seed), 8)
    return {
        "integrals": centred(arg_keys[0], (NCD, NAB), NCD ** -0.5, 0.03125, ((0, 32), (1, 32))),
        "amplitudes": heavy_noise(arg_keys[1], (N_OUTPAIR, ROWS, NCD), 1.0, 6.0, ((0, 32), (2, 32)), (2, 1, 32, 2.75)),
        "tile_live": plant((jax.random.randint(arg_keys[2], (NCD // SUB_R, NAB // SUB_C), 0, 2) < 1).astype(jnp.int32), jax.random.fold_in(arg_keys[2], 1), 0, 1),
        "batch_owner": jax.random.randint(arg_keys[3], (NB,), 0, N_OUTPAIR).astype(jnp.int32),
        "occ_energy": jnp.clip(-2.0 + 1.5 * jax.random.uniform(arg_keys[4], (NB, ROWS), jnp.float32) ** block_levels(arg_keys[4], (NB, ROWS), ((1, 32),), -0.2, 0.2), -2.0, -0.5),
        "vir_energy": jnp.clip(0.5 + 3.5 * jax.random.uniform(arg_keys[5], (NAB,), jnp.float32) ** block_levels(arg_keys[5], (NAB,), ((0, 32),), -0.2, 0.2), 0.5, 4.0),
        "swap_within": jax.random.permutation(arg_keys[6], GRP).astype(jnp.int32),
    }


def reference(integrals, amplitudes, tile_live, batch_owner, occ_energy, vir_energy, swap_within):
    batch_rows = jnp.stack([amplitudes[batch_owner[index]] for index in range(NB)])
    batch_rows = batch_rows.reshape(NB * ROWS, PAIR_IN * N_INPAIR).astype(jnp.float32)
    count = N_OUTPAIR

    def column_block(block):
        columns = lax.dynamic_slice_in_dim(integrals, block * COLS_DEV, COLS_DEV, 1)
        flags = lax.dynamic_slice_in_dim(tile_live, block * (COLS_DEV // SUB_C), COLS_DEV // SUB_C, 1)
        tile_mask = jnp.repeat(jnp.repeat(flags, SUB_R, 0), SUB_C, 1).astype(jnp.bfloat16)
        weights = (columns * tile_mask).astype(jnp.float32)
        return jnp.dot(batch_rows, weights, preferred_element_type=jnp.float32, precision=lax.Precision.HIGHEST)

    blocks = lax.map(column_block, jnp.arange(count, dtype=jnp.int32))
    summed = jnp.transpose(blocks, (1, 0, 2)).reshape(NB, ROWS, COLS_DEV * N_OUTPAIR)
    pair_grid = summed.reshape(NB, ROWS, N_OUTPAIR, N_OUTPAIR, GRP)
    swapped = jnp.take(jnp.swapaxes(pair_grid, 2, 3), swap_within, axis=4).reshape(NB, ROWS, COLS_DEV * N_OUTPAIR)
    denominator = vir_energy[None, None, :] - occ_energy[:, :, None]
    return (summed + swapped) / denominator
```

```python
import jax
import jax.numpy as jnp
from jax import lax
from jax.experimental import pallas as pl
from jax.experimental.pallas import tpu as pltpu
from jax.sharding import PartitionSpec as P

SUB_R = 256
SUB_C = 256
NB = 2
MESH = pl.DeviceIdType.MESH
LEVELS = 32000.0
F32 = jnp.float32
BF16 = jnp.bfloat16


def quantize(dst, x):
    top = jnp.maximum(jnp.max(jnp.abs(x), axis=1, keepdims=True), 1e-37)
    power = jnp.ceil(jnp.log2(top) * 8.0)
    coded = jnp.round(x * jnp.exp2(power * -0.125) * LEVELS)
    width = x.shape[1]
    dst[:, :width] = coded.astype(jnp.int32).astype(jnp.int16)
    tail = jnp.broadcast_to(power, (x.shape[0], dst.shape[1] - width))
    dst[:, width:] = tail.astype(jnp.int32).astype(jnp.int16)


def restore(src, width):
    power = src[:, width:].astype(jnp.int32).astype(F32)[:, :1]
    scale = jnp.exp2(power * 0.125) * (1.0 / LEVELS)
    return src[:, :width].astype(jnp.int32).astype(F32) * scale


def kernel(owner, mask, v_hbm, a_hbm, out, got, relay, vbuf, mask2, sel, rin, lin, rout, lout, fin, t, part,
           ysend, yrecv, zsend, zrecv,
           a_s, a_r, v_s, v_r, loc, line_s, line_r, ag_s, ag_r, y_s, y_r, z_s, z_r):
    ip = lax.axis_index("inpair")
    op = lax.axis_index("outpair")
    y, zh, c = ip // 8, (ip // 2) % 4, ip % 2
    zl, x = op // 4, op % 4
    xp, xm, xo = (x + 1) % 4, (x + 3) % 4, (x + 2) % 4
    right, left = zl * 4 + xp, zl * 4 + xm
    partner = ip + 1 - 2 * c
    other = 1 - c
    y_up, y_down = (ip + 8) % 32, (ip + 24) % 32
    z_up, z_down = y * 8 + ((zh + 1) % 4) * 2 + c, y * 8 + ((zh + 3) % 4) * 2 + c
    width = v_hbm.shape[1]

    def send(src, dst, s_sem, r_sem, i, o):
        return pltpu.make_async_remote_copy(src_ref=src, dst_ref=dst, send_sem=s_sem, recv_sem=r_sem,
                                            device_id={"inpair": i, "outpair": o}, device_id_type=MESH)

    barrier = pltpu.get_barrier_semaphore()

    def greet(i, o):
        pl.semaphore_signal(barrier, inc=1, device_id={"inpair": i, "outpair": o}, device_id_type=MESH)

    for i in (z_up, z_down, y_up, y_down, partner):
        greet(i, op)
    for o in (right, left):
        greet(ip, o)
        greet(partner, o)

    @pl.when(zl > 0)
    def _():
        greet(ip, op - 4)

    @pl.when(zl < 7)
    def _():
        greet(ip, op + 4)

    load_v = pltpu.make_async_copy(v_hbm, vbuf.at[c], loc.at[0])
    load_v.start()
    load_a = pltpu.make_async_copy(a_hbm.at[0, pl.ds(pl.multiple_of(x * 128, 128), 128)], got.at[x], loc.at[1])
    load_a.start()

    @pl.when(zl == 0)
    def _():
        rin[...] = jnp.zeros_like(rin)

    @pl.when(zl == 7)
    def _():
        lin[...] = jnp.zeros_like(lin)

    pl.semaphore_wait(barrier, 9 + jnp.where(zl > 0, 1, 0) + jnp.where(zl < 7, 1, 0))

    def rows(q, start, n):
        return a_hbm.at[0, pl.ds(pl.multiple_of(q * 128 + start, 64), n)]

    relay_r = send(rows(xo, 0, 64), relay.at[0], a_s.at[0], a_r.at[0], ip, right)
    relay_l = send(rows(xo, 64, 64), relay.at[1], a_s.at[1], a_r.at[1], ip, left)
    full_r = send(rows(xp, 0, 128), got.at[x], a_s.at[2], a_r.at[2], ip, right)
    full_l = send(rows(xm, 0, 128), got.at[x], a_s.at[3], a_r.at[3], ip, left)
    on_r = send(relay.at[0], got.at[xm, pl.ds(0, 64)], a_s.at[4], a_r.at[4], ip, right)
    on_l = send(relay.at[1], got.at[xp, pl.ds(64, 64)], a_s.at[5], a_r.at[5], ip, left)
    for copy in (relay_r, relay_l, full_r, full_l):
        copy.start()
    swap_m = send(mask, mask2, v_s.at[0], v_r.at[0], partner, op)
    swap_v = send(v_hbm, vbuf.at[c], v_s.at[1], v_r.at[1], partner, op)
    swap_m.start()
    swap_v.start()
    relay_r.wait_recv()
    on_r.start()
    relay_l.wait_recv()
    on_l.start()

    def mask_half(half, m):
        for a in range(width // SUB_C):
            at = pl.ds(a * SUB_R, SUB_R)
            vbuf[half, at, :] = vbuf[half, at, :] * m[a:a + 1, :].astype(BF16)

    load_v.wait()
    mask_half(c, mask)
    load_a.wait()
    for copy in (full_r, full_l, on_r, on_l):
        copy.wait_recv()

    def select(k, carry):
        row = (k % 4) * 32 + (c + (k // 4) * (1 - 2 * c)) * 16
        for b in range(NB):
            holder = owner[b]
            here = jnp.where((holder >> 2) == zl, 1.0, 0.0)
            value = got[holder & 3, pl.ds(pl.multiple_of(row, 16), 16), :]
            sel[k, b * 16:(b + 1) * 16, :] = (value.astype(F32) * here).astype(BF16)
        return carry

    lax.fori_loop(0, 8, select, 0)

    far = jnp.maximum(zl, 7 - zl)

    def line_r_copy(k):
        return send(rout.at[k], rin.at[k], line_s.at[0, k], line_r.at[0, k], ip, op + 4)

    def line_l_copy(k):
        return send(lout.at[k], lin.at[k], line_s.at[1, k], line_r.at[1, k], ip, op - 4)

    def ag_copies(k):
        part_k = k // 4
        core = c + part_k * (1 - 2 * c)
        dst = t.at[c, x, pl.ds(pl.multiple_of((k % 4) * 32, 32), 32)]
        to = ip - c + core
        return (send(fin.at[k], dst, ag_s.at[0, k], ag_r.at[0, k], to, right),
                send(fin.at[k], dst, ag_s.at[1, k], ag_r.at[1, k], to, left))

    def pass_on(k, direction):
        half = c + (k // 4) * (1 - 2 * c)
        at = pl.ds(pl.multiple_of((k % 4) * 32, 32), 32)
        if direction == 0:
            return send(t.at[half, xm, at], t.at[half, xm, at], ag_s.at[2, k], ag_r.at[2, k], ip, right)
        return send(t.at[half, xp, at], t.at[half, xp, at], ag_s.at[2, k], ag_r.at[2, k], ip, left)

    def to_partner(k):
        dst = t.at[c, x, pl.ds(pl.multiple_of((k % 4) * 32, 32), 32)]
        return send(fin.at[k], dst, ag_s.at[3, k], ag_r.at[3, k], partner, op)

    lag = 2

    def line(step, carry):
        kr = step - zl

        @pl.when(jnp.logical_and(kr >= 0, kr < 8))
        def _():
            @pl.when(zl > 0)
            def _():
                line_r_copy(kr).wait_recv()

            @pl.when(zl < 7)
            def _():
                rout[kr] = sel[kr] + rin[kr]
                line_r_copy(kr).start()

        kl = step - (7 - zl)

        @pl.when(jnp.logical_and(kl >= 0, kl < 8))
        def _():
            @pl.when(zl < 7)
            def _():
                line_l_copy(kl).wait_recv()

            @pl.when(zl > 0)
            def _():
                lout[kl] = sel[kl] + lin[kl]
                line_l_copy(kl).start()

        kf = step - far

        @pl.when(jnp.logical_and(kf >= 0, kf < 8))
        def _():
            value = sel[kf] + rin[kf] + lin[kf]
            fin[kf] = value

            @pl.when(kf < 4)
            def _():
                t[c, x, pl.ds(pl.multiple_of((kf % 4) * 32, 32), 32), :] = value

            @pl.when(kf >= 4)
            def _():
                to_partner(kf).start()

            for copy in ag_copies(kf):
                copy.start()

        kp = step - far - lag

        @pl.when(jnp.logical_and(kp >= 0, kp < 8))
        def _():
            @pl.when(kp % 2 == 0)
            def _():
                ag_copies(kp)[0].wait_recv()
                pass_on(kp, 0).start()

            @pl.when(kp % 2 == 1)
            def _():
                ag_copies(kp)[1].wait_recv()
                pass_on(kp, 1).start()

        return carry

    lax.fori_loop(0, 15 + lag, line, 0)

    swap_m.wait_recv()
    swap_v.wait_recv()
    mask_half(other, mask2)

    def arrived(k, carry):
        @pl.when(k % 2 == 0)
        def _():
            ag_copies(k)[1].wait_recv()
            pass_on(k, 0).wait_recv()

        @pl.when(k % 2 == 1)
        def _():
            ag_copies(k)[0].wait_recv()
            pass_on(k, 1).wait_recv()

        @pl.when(k >= 4)
        def _():
            to_partner(k).wait_recv()

        return carry

    lax.fori_loop(0, 8, arrived, 0)

    def product(n, carry):
        at = pl.ds(pl.multiple_of(n * 256, 256), 256)
        total = jnp.dot(t[0].reshape(512, 1024), vbuf[0, :, at], preferred_element_type=F32)
        total = total + jnp.dot(t[1].reshape(512, 1024), vbuf[1, :, at], preferred_element_type=F32)
        part[:, :, at] = total.reshape(4, 128, 256)
        return carry

    lax.fori_loop(0, width // 256, product, 0)

    def tree(piece, sendbuf, recvbuf, s_sem, r_sem, up, down):
        def copy(m, to):
            return send(sendbuf.at[m], recvbuf.at[m], s_sem.at[m], r_sem.at[m], to, op)

        copies = [copy(m, (up, down)[m % 2]) for m in (0, 1, 2, 3, 4, 5)]
        first = ((2, 0), (2, 1), (1, 1), (3, 0))
        for m in range(4):
            quantize(sendbuf.at[m], piece(*first[m]))
            copies[m].start()
        for m, which in ((4, (1, 0)), (5, (3, 1))):
            copies[m - 4].wait_recv()
            quantize(sendbuf.at[m], piece(*which) + restore(recvbuf.at[m - 4], width))
            copies[m].start()
        return copies, ((3, 4), (2, 5))

    def y_piece(d, h):
        return part[(y + d) % 4, h * 64:(h + 1) * 64, :]

    y_copies, order = tree(y_piece, ysend, yrecv, y_s, y_r, y_up, y_down)
    for h in range(2):
        value = y_piece(0, h)
        for m in order[h]:
            y_copies[m].wait_recv()
            value = value + restore(yrecv.at[m], width)
        part[y, h * 64:(h + 1) * 64, :] = value

    def z_piece(d, h):
        return part[y, pl.ds(pl.multiple_of(((zh + d) % 4) * 32 + h * 16, 16), 16), :]

    z_copies, order = tree(z_piece, zsend, zrecv, z_s, z_r, z_up, z_down)
    for h in range(2):
        value = z_piece(0, h)
        for m in order[h]:
            z_copies[m].wait_recv()
            value = value + restore(zrecv.at[m], width)
        out[h] = value

    for copy in (relay_r, relay_l, full_r, full_l, on_r, on_l, swap_m, swap_v, *y_copies, *z_copies):
        copy.wait_send()

    def drained(k, carry):
        @pl.when(zl < 7)
        def _():
            line_r_copy(k).wait_send()

        @pl.when(zl > 0)
        def _():
            line_l_copy(k).wait_send()

        for copy in ag_copies(k):
            copy.wait_send()

        @pl.when(k % 2 == 0)
        def _():
            pass_on(k, 0).wait_send()

        @pl.when(k % 2 == 1)
        def _():
            pass_on(k, 1).wait_send()

        @pl.when(k >= 4)
        def _():
            to_partner(k).wait_send()

        return carry

    lax.fori_loop(0, 8, drained, 0)


def contract(owner, mask, integrals, amplitudes):
    any_spec = pl.BlockSpec(memory_space=pl.ANY)
    vmem = pl.BlockSpec(memory_space=pltpu.VMEM)
    dma = pltpu.SemaphoreType.DMA
    return pl.pallas_call(
        kernel,
        out_shape=jax.ShapeDtypeStruct((NB, 16, 1024), F32),
        in_specs=[pl.BlockSpec(memory_space=pltpu.SMEM), vmem, any_spec, any_spec],
        out_specs=vmem,
        scratch_shapes=[
            pltpu.VMEM((4, 128, 1024), BF16),
            pltpu.VMEM((2, 64, 1024), BF16),
            pltpu.VMEM((2, 1024, 1024), BF16),
            pltpu.VMEM((8, 1024), F32),
            *[pltpu.VMEM((8, 32, 1024), BF16)] * 6,
            pltpu.VMEM((2, 4, 128, 1024), BF16),
            pltpu.VMEM((4, 128, 1024), F32),
            *[pltpu.VMEM((6, 64, 1152), jnp.int16)] * 2,
            *[pltpu.VMEM((6, 16, 1152), jnp.int16)] * 2,
            dma((6,)), dma((6,)), dma((2,)), dma((2,)), dma((2,)),
            dma((2, 8)), dma((2, 8)), dma((4, 8)), dma((4, 8)),
            dma((6,)), dma((6,)), dma((6,)), dma((6,)),
        ],
        compiler_params=pltpu.CompilerParams(collective_id=0, has_side_effects=True, vmem_limit_bytes=48 * 1024 * 1024),
    )(owner, mask, integrals, amplitudes)


def on_device(integrals, amplitudes, tile_live, batch_owner, occ_energy, vir_energy, swap_within):
    parties = lax.axis_size("outpair")
    mask = jnp.repeat(jnp.pad(tile_live, ((0, 4), (0, 0))), SUB_C, 1).astype(F32)
    summed = contract(batch_owner, mask, integrals, amplitudes)
    local_rows = summed.shape[1]
    width = summed.shape[2]
    pair_grid = summed.reshape(NB, local_rows, parties, width // parties)
    received = lax.all_to_all(pair_grid, "outpair", split_axis=2, concat_axis=2, tiled=True)
    swapped = jnp.take(received, swap_within, axis=3).reshape(NB, local_rows, width)
    denominator = vir_energy[None, None, :] - occ_energy[:, :, None]
    return (summed + swapped) / denominator


def solution(mesh):
    return jax.shard_map(
        on_device,
        mesh=mesh,
        in_specs=(
            P("inpair", "outpair"),
            P("outpair", None, "inpair"),
            P("inpair", "outpair"),
            P(),
            P(None, "inpair"),
            P("outpair"),
            P(),
        ),
        out_specs=P(None, "inpair", "outpair"),
        check_vma=False,
    )
```

```python
import jax
import jax.numpy as jnp
from jax import lax
from jax.experimental import pallas as pl
from jax.experimental.pallas import tpu as pltpu
from jax.sharding import PartitionSpec as P

SUB_R = 256
SUB_C = 256
NB = 2
GRP = 32
CH = 16
SUBS = 32 // CH
NCH = 8 * SUBS
LAG = 5
HOP = 4
VMEM_LIMIT = 62 * 1024 * 1024
MESH = pl.DeviceIdType.MESH
LEVELS = 32000.0
F32 = jnp.float32
BF16 = jnp.bfloat16


def quantize(dst, x):
    top = jnp.maximum(jnp.max(jnp.abs(x), axis=1, keepdims=True), 1e-37)
    power = jnp.ceil(jnp.log2(top) * 8.0)
    coded = jnp.round(x * jnp.exp2(power * -0.125) * LEVELS)
    width = x.shape[1]
    dst[:, :width] = coded.astype(jnp.int32).astype(jnp.int16)
    tail = jnp.broadcast_to(power, (x.shape[0], dst.shape[1] - width))
    dst[:, width:] = tail.astype(jnp.int32).astype(jnp.int16)


def restore(src, width):
    power = src[:, width:].astype(jnp.int32).astype(F32)[:, :1]
    scale = jnp.exp2(power * 0.125) * (1.0 / LEVELS)
    return src[:, :width].astype(jnp.int32).astype(F32) * scale


def regroup(parts):
    lane = lax.broadcasted_iota(jnp.int32, parts[0].shape, 1) // GRP
    out = []
    for i in range(4):
        value = parts[i]
        for n in range(4):
            if n != i:
                value = jnp.where(lane == n, pltpu.roll(parts[n], ((n - i) * GRP) % 128, axis=1), value)
        out.append(value)
    return out


def kernel(owner, live, swap, v_hbm, a_hbm, out, mask, got, relay, vbuf, mask2, sel, rin, lin, rout, lout, fin, t, part,
           ysend, yrecv, zsend, zrecv, mine, d1, d2s, d2r,
           a_s, a_r, v_s, v_r, loc, line_s, line_r, ag_s, ag_r, y_s, y_r, z_s, z_r, d1_s, d1_r, d2_sem, d2_rem):
    ip = lax.axis_index("inpair")
    op = lax.axis_index("outpair")
    y, zh, c = ip // 8, (ip // 2) % 4, ip % 2
    zl, x = op // 4, op % 4
    xp, xm, xo = (x + 1) % 4, (x + 3) % 4, (x + 2) % 4
    right, left, across = zl * 4 + xp, zl * 4 + xm, zl * 4 + xo
    partner = ip + 1 - 2 * c
    other = 1 - c
    y_up, y_down = (ip + 8) % 32, (ip + 24) % 32
    z_up, z_down = y * 8 + ((zh + 1) % 4) * 2 + c, y * 8 + ((zh + 3) % 4) * 2 + c
    width = v_hbm.shape[1]

    def send(src, dst, s_sem, r_sem, i, o):
        return pltpu.make_async_remote_copy(src_ref=src, dst_ref=dst, send_sem=s_sem, recv_sem=r_sem,
                                            device_id={"inpair": i, "outpair": o}, device_id_type=MESH)

    def along(n):
        return ((zl + n) % 8) * 4 + x

    barrier = pltpu.get_barrier_semaphore()

    def greet(i, o):
        pl.semaphore_signal(barrier, inc=1, device_id={"inpair": i, "outpair": o}, device_id_type=MESH)

    for i in (z_up, z_down):
        greet(i, op)
    for n in range(1, 8):
        greet(ip, along(n))
    for i in (y_up, y_down, partner):
        greet(i, op)
    greet(ip, across)
    for o in (right, left):
        greet(ip, o)
        greet(partner, o)

    for a in range(4):
        for b in range(width // SUB_C):
            mask[a:a + 1, b * SUB_C:(b + 1) * SUB_C] = jnp.full((1, SUB_C), live[a, b].astype(F32), F32)
    mask[4:8, :] = jnp.zeros((4, width), F32)

    load_v = pltpu.make_async_copy(v_hbm, vbuf.at[c], loc.at[0])
    load_v.start()
    load_a = pltpu.make_async_copy(a_hbm.at[0, pl.ds(pl.multiple_of(x * 128, 128), 128)], got.at[x], loc.at[1])
    load_a.start()

    @pl.when(zl == 0)
    def _():
        rin[...] = jnp.zeros_like(rin)

    @pl.when(zl == 7)
    def _():
        lin[...] = jnp.zeros_like(lin)

    pl.semaphore_wait(barrier, 17)

    def quarter(j):
        return (zh + 2 - j + jnp.where(j == 2, 3, 0) + jnp.where(j == 3, 1, 0) + 4) % 4

    def rows(q, j, start, n):
        return a_hbm.at[0, pl.ds(pl.multiple_of(q * 128 + quarter(j) * 32 + start, 16), n)]

    def in_got(q, j, start, n):
        return got.at[q, pl.ds(pl.multiple_of(quarter(j) * 32 + start, 16), n)]

    def relays(j):
        return (send(rows(xo, j, 0, 16), relay.at[0, j], a_s.at[0, j], a_r.at[0, j], ip, right),
                send(rows(xo, j, 16, 16), relay.at[1, j], a_s.at[1, j], a_r.at[1, j], ip, left))

    def fulls(j):
        return (send(rows(xp, j, 0, 32), in_got(x, j, 0, 32), a_s.at[2, j], a_r.at[2, j], ip, right),
                send(rows(xm, j, 0, 32), in_got(x, j, 0, 32), a_s.at[3, j], a_r.at[3, j], ip, left))

    def onward(j):
        return (send(relay.at[0, j], in_got(xm, j, 0, 16), a_s.at[4, j], a_r.at[4, j], ip, right),
                send(relay.at[1, j], in_got(xp, j, 16, 16), a_s.at[5, j], a_r.at[5, j], ip, left))

    def start_relays(j, carry):
        for copy in relays(j):
            copy.start()
        return carry

    def start_fulls(j, carry):
        for copy in fulls(j):
            copy.start()
        return carry

    def start_onward(j, carry):
        for copy, was in zip(onward(j), relays(j)):
            was.wait_recv()
            copy.start()
        return carry

    lax.fori_loop(0, 4, start_relays, 0)
    lax.fori_loop(0, 2, start_fulls, 0)
    swap_m = send(mask, mask2, v_s.at[0], v_r.at[0], partner, op)
    swap_v = send(v_hbm, vbuf.at[c], v_s.at[1], v_r.at[1], partner, op)
    swap_m.start()
    swap_v.start()

    def mask_half(half, m):
        for a in range(width // SUB_C):
            at = pl.ds(a * SUB_R, SUB_R)
            vbuf[half, at, :] = vbuf[half, at, :] * m[a:a + 1, :].astype(BF16)

    load_v.wait()
    mask_half(c, mask)
    lax.fori_loop(0, 2, start_onward, 0)

    def start_rest(j, carry):
        start_fulls(j, 0)
        return start_onward(j, carry)

    lax.fori_loop(2, 4, start_rest, 0)
    load_a.wait()
    swap_m.wait_recv()
    swap_v.wait_recv()
    mask_half(other, mask2)

    def place(k):
        sub, rel = k % SUBS, (k // SUBS) % 2
        return quarter(k // (2 * SUBS)), rel, sub, c + rel * (1 - 2 * c)

    def select(j):
        for copy in (*fulls(j), *onward(j)):
            copy.wait_recv()
        for n in range(2 * SUBS):
            core = c + (n // SUBS) * (1 - 2 * c)
            for part_b in range(CH // 16):
                b = (n % SUBS) if SUBS == 2 else part_b
                holder = owner[b]
                at = pl.ds(pl.multiple_of(quarter(j) * 32 + core * 16, 16), 16)
                value = jnp.zeros((16, width), F32)
                for held in range(4):
                    value = value + got[held, at, :].astype(F32) * jnp.where(holder == zl * 4 + held, 1.0, 0.0)
                sel[j * 2 * SUBS + n, part_b * 16:(part_b + 1) * 16, :] = value.astype(BF16)

    far = HOP * jnp.maximum(zl, 7 - zl)
    near = HOP * jnp.minimum(zl, 7 - zl)

    def line_r_copy(k):
        return send(rout.at[k], rin.at[k], line_s.at[0, k], line_r.at[0, k], ip, op + 4)

    def line_l_copy(k):
        return send(lout.at[k], lin.at[k], line_s.at[1, k], line_r.at[1, k], ip, op - 4)

    def in_t(k, src_x):
        q, _, sub, _ = place(k)
        return q, pl.ds(pl.multiple_of(src_x * 32 + sub * 16, 16), CH)

    def ag_copies(k):
        q, at = in_t(k, x)
        core = place(k)[3]
        dst = t.at[c, q, at]
        to = ip - c + core
        return (send(fin.at[k], dst, ag_s.at[0, k], ag_r.at[0, k], to, right),
                send(fin.at[k], dst, ag_s.at[1, k], ag_r.at[1, k], to, left))

    def pass_on(k, rel):
        if rel == 0:
            q, at = in_t(k, xm)
            return send(t.at[c, q, at], t.at[c, q, at], ag_s.at[2, k], ag_r.at[2, k], ip, right)
        q, at = in_t(k, xp)
        return send(t.at[other, q, at], t.at[other, q, at], ag_s.at[2, k], ag_r.at[2, k], ip, left)

    def to_partner(k):
        q, at = in_t(k, x)
        return send(fin.at[k], t.at[c, q, at], ag_s.at[3, k], ag_r.at[3, k], partner, op)

    def by_kind(k, even, odd):
        rel = (k // SUBS) % 2

        @pl.when(rel == 0)
        def _():
            even()

        @pl.when(rel == 1)
        def _():
            odd()

    def line(step, carry):
        kq = step - near

        @pl.when(jnp.logical_and(jnp.logical_and(kq >= 0, kq < NCH), kq % (2 * SUBS) == 0))
        def _():
            select(kq // (2 * SUBS))

        kr = step - HOP * zl

        @pl.when(jnp.logical_and(kr >= 0, kr < NCH))
        def _():
            @pl.when(zl > 0)
            def _():
                line_r_copy(kr).wait_recv()

            @pl.when(zl < 7)
            def _():
                rout[kr] = sel[kr] + rin[kr]
                line_r_copy(kr).start()

        kl = step - HOP * (7 - zl)

        @pl.when(jnp.logical_and(kl >= 0, kl < NCH))
        def _():
            @pl.when(zl < 7)
            def _():
                line_l_copy(kl).wait_recv()

            @pl.when(zl > 0)
            def _():
                lout[kl] = sel[kl] + lin[kl]
                line_l_copy(kl).start()

        kf = step - far

        @pl.when(jnp.logical_and(kf >= 0, kf < NCH))
        def _():
            value = sel[kf] + rin[kf] + lin[kf]
            fin[kf] = value

            def keep():
                q, at = in_t(kf, x)
                t[c, q, at, :] = value

            by_kind(kf, keep, lambda: to_partner(kf).start())
            for copy in ag_copies(kf):
                copy.start()

        kx = step - far - LAG
        kp = kx - kx // 3

        @pl.when(jnp.logical_and(kx >= 0, kx % 3 != 2))
        def _():
            forward(kp, 0)

        return carry

    def forward(k, carry):
        def even():
            ag_copies(k)[0].wait_recv()
            pass_on(k, 0).start()

        def odd():
            ag_copies(k)[1].wait_recv()
            pass_on(k, 1).start()

        by_kind(k, even, odd)
        return carry

    lax.fori_loop(0, far + NCH, line, 0)
    done = NCH - LAG - (NCH - LAG) // 3

    def arrived(k, carry):
        def even():
            ag_copies(k)[1].wait_recv()
            pass_on(k, 0).wait_recv()

        def odd():
            ag_copies(k)[0].wait_recv()
            pass_on(k, 1).wait_recv()
            to_partner(k).wait_recv()

        by_kind(k, even, odd)
        return carry

    def zq(j):
        return (zh + (2, 1, 3, 0)[j]) % 4

    def product(j):
        lax.fori_loop(2 * SUBS * j, 2 * SUBS * (j + 1), arrived, 0)
        q = zq(j)

        def columns(n, carry):
            at = pl.ds(pl.multiple_of(n * 256, 256), 256)
            total = jnp.dot(t[0, q], vbuf[0, :, at], preferred_element_type=F32)
            total = total + jnp.dot(t[1, q], vbuf[1, :, at], preferred_element_type=F32)
            part[q, :, at] = total
            return carry

        lax.fori_loop(0, width // 256, columns, 0)

    FIRST = ((2, 0), (2, 1), (1, 1), (3, 0))
    SECOND = {4: (1, 0), 5: (3, 1)}
    LAST = ((3, 4), (2, 5))

    def y_copy(j, m):
        return send(ysend.at[j, m], yrecv.at[j, m], y_s.at[j, m], y_r.at[j, m], (y_up, y_down)[m % 2], op)

    def y_piece(j, d, h):
        return part[zq(j), pl.ds(pl.multiple_of(((y + d) % 4) * 32 + h * 16, 16), 16), :]

    def y_first(j):
        for m in range(4):
            quantize(ysend.at[j, m], y_piece(j, *FIRST[m]))
            y_copy(j, m).start()

    def y_second(j):
        for m in (4, 5):
            y_copy(j, m - 4).wait_recv()
            quantize(ysend.at[j, m], y_piece(j, *SECOND[m]) + restore(yrecv.at[j, m - 4], width))
            y_copy(j, m).start()

    def y_last(j):
        values = []
        for h in range(2):
            value = y_piece(j, 0, h)
            for m in LAST[h]:
                y_copy(j, m).wait_recv()
                value = value + restore(yrecv.at[j, m], width)
            values.append(value)
        return values

    def z_copy(m):
        return send(zsend.at[m], zrecv.at[m], z_s.at[m], z_r.at[m], (z_up, z_down)[m % 2], op)

    def z_send(m, value):
        quantize(zsend.at[m], value)
        z_copy(m).start()

    def z_join(value, m):
        z_copy(m).wait_recv()
        return value + restore(zrecv.at[m], width)

    product(0)
    y_first(0)
    lax.fori_loop(done, done + 4, forward, 0)
    product(1)
    y_first(1)
    y_second(0)
    lax.fori_loop(done + 4, NCH, forward, 0)
    product(2)
    y_first(2)
    y_second(1)
    opposite = y_last(0)
    z_send(0, opposite[0])
    z_send(1, opposite[1])
    product(3)
    y_first(3)
    y_second(2)
    above = y_last(1)
    z_send(2, above[1])
    y_second(3)
    below = y_last(2)
    z_send(3, below[0])
    part[zq(1), 0:16, :] = above[0]
    part[zq(2), 0:16, :] = below[1]
    own = y_last(3)
    mine[0:16, :] = own[0]
    mine[16:32, :] = own[1]
    z_send(4, z_join(part[zq(1), 0:16, :], 0))
    z_send(5, z_join(part[zq(2), 0:16, :], 1))
    for h in range(2):
        value = mine[h * 16:(h + 1) * 16, :]
        for m in LAST[h]:
            value = z_join(value, m)
        mine[h * 16:(h + 1) * 16, :] = value

    def d1_copy(n):
        at = pl.ds(pl.multiple_of(((zl + n) % 8) * 128, 128), 128)
        return send(mine.at[:, at], d1.at[zl], d1_s.at[n], d1_r.at[n], ip, along(n))

    for n in (4, 3, 5, 2, 6, 1, 7):
        d1_copy(n).start()
    d1[zl] = mine[:, pl.ds(pl.multiple_of(zl * 128, 128), 128)]
    for n in range(1, 8):
        d1_copy(n).wait_recv()
    packed = regroup([d1[:, r * 8:(r + 1) * 8, :].reshape(64, 128) for r in range(4)])
    for i in range(4):
        d2s[i] = packed[i]

    def d2_copy(n, to):
        return send(d2s.at[(x + n) % 4], d2r.at[x], d2_sem.at[n], d2_rem.at[n], ip, to)

    d2_copies = [d2_copy(2, across), d2_copy(1, right), d2_copy(3, left)]
    for copy in d2_copies:
        copy.start()
    d2r[x] = d2s[x]
    row = lax.broadcasted_iota(jnp.int32, (128, 128), 0)
    column = lax.broadcasted_iota(jnp.int32, (8, 128), 1)
    target = jnp.zeros((8, 128), jnp.int32)
    for g in range(GRP):
        target = jnp.where(column % GRP == g, swap[g] + (column // GRP) * GRP, target)
    pick = jnp.where(row == target[0:1, :], 1.0, 0.0).astype(BF16)
    for copy in d2_copies:
        copy.wait_recv()
    faced = regroup([d2r[i] for i in range(4)])
    for r in range(4):
        rest = faced[r]
        moved = jnp.zeros((64, 128), F32)
        for _ in range(3):
            piece = rest.astype(BF16)
            rest = rest - piece.astype(F32)
            moved = moved + jnp.dot(piece, pick, preferred_element_type=F32)
        for n in range(8):
            out[r // 2, (r % 2) * 8:(r % 2) * 8 + 8, n * 128:(n + 1) * 128] = (
                mine[r * 8:(r + 1) * 8, n * 128:(n + 1) * 128] + moved[n * 8:(n + 1) * 8, :])

    for copy in (swap_m, swap_v, *d2_copies):
        copy.wait_send()
    for n in range(1, 8):
        d1_copy(n).wait_send()
    for m in range(6):
        z_copy(m).wait_send()

    def drained_quarter(j, carry):
        for copy in (*relays(j), *fulls(j), *onward(j)):
            copy.wait_send()
        for m in range(6):
            y_copy(j, m).wait_send()
        return carry

    lax.fori_loop(0, 4, drained_quarter, 0)

    def drained(k, carry):
        @pl.when(zl < 7)
        def _():
            line_r_copy(k).wait_send()

        @pl.when(zl > 0)
        def _():
            line_l_copy(k).wait_send()

        for copy in ag_copies(k):
            copy.wait_send()

        def odd():
            pass_on(k, 1).wait_send()
            to_partner(k).wait_send()

        by_kind(k, lambda: pass_on(k, 0).wait_send(), odd)
        return carry

    lax.fori_loop(0, NCH, drained, 0)


def contract(owner, live, swap, integrals, amplitudes):
    any_spec = pl.BlockSpec(memory_space=pl.ANY)
    vmem = pl.BlockSpec(memory_space=pltpu.VMEM)
    dma = pltpu.SemaphoreType.DMA
    return pl.pallas_call(
        kernel,
        out_shape=jax.ShapeDtypeStruct((NB, 16, 1024), F32),
        in_specs=[pl.BlockSpec(memory_space=pltpu.SMEM)] * 3 + [any_spec, any_spec],
        out_specs=vmem,
        scratch_shapes=[
            pltpu.VMEM((8, 1024), F32),
            pltpu.VMEM((4, 128, 1024), BF16),
            pltpu.VMEM((2, 4, 16, 1024), BF16),
            pltpu.VMEM((2, 1024, 1024), BF16),
            pltpu.VMEM((8, 1024), F32),
            *[pltpu.VMEM((NCH, CH, 1024), BF16)] * 6,
            pltpu.VMEM((2, 4, 128, 1024), BF16),
            pltpu.VMEM((4, 128, 1024), F32),
            *[pltpu.VMEM((4, 6, 16, 1152), jnp.int16)] * 2,
            *[pltpu.VMEM((6, 16, 1152), jnp.int16)] * 2,
            pltpu.VMEM((32, 1024), F32),
            pltpu.VMEM((8, 32, 128), F32),
            *[pltpu.VMEM((4, 64, 128), F32)] * 2,
            dma((6, 4)), dma((6, 4)), dma((2,)), dma((2,)), dma((2,)),
            dma((2, NCH)), dma((2, NCH)), dma((4, NCH)), dma((4, NCH)),
            dma((4, 6)), dma((4, 6)), dma((6,)), dma((6,)),
            dma((8,)), dma((8,)), dma((4,)), dma((4,)),
        ],
        compiler_params=pltpu.CompilerParams(collective_id=0, has_side_effects=True,
                                             vmem_limit_bytes=VMEM_LIMIT),
    )(owner, live, swap, integrals, amplitudes)


def on_device(integrals, amplitudes, tile_live, batch_owner, occ_energy, vir_energy, swap_within):
    both = contract(batch_owner, tile_live, swap_within, integrals, amplitudes)
    return both / (vir_energy[None, None, :] - occ_energy[:, :, None])


def solution(mesh):
    return jax.shard_map(
        on_device,
        mesh=mesh,
        in_specs=(
            P("inpair", "outpair"),
            P("outpair", None, "inpair"),
            P("inpair", "outpair"),
            P(),
            P(None, "inpair"),
            P("outpair"),
            P(),
        ),
        out_specs=P(None, "inpair", "outpair"),
        check_vma=False,
    )
```

```python
import jax
import jax.numpy as jnp
from jax import lax
from jax.experimental import pallas as pl
from jax.experimental.pallas import tpu as pltpu
from jax.sharding import PartitionSpec as P

SUB_R = 256
SUB_C = 256
NB = 2
GRP = 32
CH = 16
SUBS = 32 // CH
NCH = 8 * SUBS
LAG = 5
HOP = 4
VMEM_LIMIT = 62 * 1024 * 1024
MESH = pl.DeviceIdType.MESH
LEVELS = 32000.0
F32 = jnp.float32
BF16 = jnp.bfloat16


def quantize(dst, x):
    top = jnp.maximum(jnp.max(jnp.abs(x), axis=1, keepdims=True), 1e-37)
    power = jnp.ceil(jnp.log2(top) * 8.0)
    coded = jnp.round(x * jnp.exp2(power * -0.125) * LEVELS)
    width = x.shape[1]
    dst[:, :width] = coded.astype(jnp.int32).astype(jnp.int16)
    tail = jnp.broadcast_to(power, (x.shape[0], dst.shape[1] - width))
    dst[:, width:] = tail.astype(jnp.int32).astype(jnp.int16)


def restore(src, width):
    power = src[:, width:].astype(jnp.int32).astype(F32)[:, :1]
    scale = jnp.exp2(power * 0.125) * (1.0 / LEVELS)
    return src[:, :width].astype(jnp.int32).astype(F32) * scale


def regroup(parts):
    lane = lax.broadcasted_iota(jnp.int32, parts[0].shape, 1) // GRP
    out = []
    for i in range(4):
        value = parts[i]
        for n in range(4):
            if n != i:
                value = jnp.where(lane == n, pltpu.roll(parts[n], ((n - i) * GRP) % 128, axis=1), value)
        out.append(value)
    return out


def kernel(owner, live, swap, v_hbm, a_hbm, out, mask, got, relay, vbuf, mask2, sel, rin, lin, rout, lout, fin, t, part,
           ysend, yrecv, zsend, zrecv, mine, d1, d2s, d2r,
           a_s, a_r, v_s, v_r, loc, line_s, line_r, ag_s, ag_r, y_s, y_r, z_s, z_r, d1_s, d1_r, d2_sem, d2_rem):
    ip = lax.axis_index("inpair")
    op = lax.axis_index("outpair")
    y, zh, c = ip // 8, (ip // 2) % 4, ip % 2
    zl, x = op // 4, op % 4
    xp, xm, xo = (x + 1) % 4, (x + 3) % 4, (x + 2) % 4
    right, left, across = zl * 4 + xp, zl * 4 + xm, zl * 4 + xo
    partner = ip + 1 - 2 * c
    other = 1 - c
    y_up, y_down = (ip + 8) % 32, (ip + 24) % 32
    z_up, z_down = y * 8 + ((zh + 1) % 4) * 2 + c, y * 8 + ((zh + 3) % 4) * 2 + c
    width = v_hbm.shape[1]

    def send(src, dst, s_sem, r_sem, i, o):
        return pltpu.make_async_remote_copy(src_ref=src, dst_ref=dst, send_sem=s_sem, recv_sem=r_sem,
                                            device_id={"inpair": i, "outpair": o}, device_id_type=MESH)

    def along(n):
        return ((zl + n) % 8) * 4 + x

    barrier = pltpu.get_barrier_semaphore()

    def greet(i, o):
        pl.semaphore_signal(barrier, inc=1, device_id={"inpair": i, "outpair": o}, device_id_type=MESH)

    for i in (z_up, z_down):
        greet(i, op)
    for n in range(1, 8):
        greet(ip, along(n))
    for i in (y_up, y_down, partner):
        greet(i, op)
    greet(ip, across)
    greet(partner, across)
    for o in (right, left):
        greet(ip, o)
        greet(partner, o)

    for a in range(4):
        for b in range(width // SUB_C):
            mask[a:a + 1, b * SUB_C:(b + 1) * SUB_C] = jnp.full((1, SUB_C), live[a, b].astype(F32), F32)
    mask[4:8, :] = jnp.zeros((4, width), F32)

    load_v = pltpu.make_async_copy(v_hbm, vbuf.at[c], loc.at[0])
    load_v.start()
    load_a = pltpu.make_async_copy(a_hbm.at[0, pl.ds(pl.multiple_of(x * 128, 128), 128)], got.at[x], loc.at[1])
    load_a.start()

    @pl.when(zl == 0)
    def _():
        rin[...] = jnp.zeros_like(rin)

    @pl.when(zl == 7)
    def _():
        lin[...] = jnp.zeros_like(lin)

    pl.semaphore_wait(barrier, 18)

    def quarter(j):
        return (zh + 2 - j + jnp.where(j == 2, 3, 0) + jnp.where(j == 3, 1, 0) + 4) % 4

    def rows(q, j, start, n):
        return a_hbm.at[0, pl.ds(pl.multiple_of(q * 128 + quarter(j) * 32 + start, 16), n)]

    def in_got(q, j, start, n):
        return got.at[q, pl.ds(pl.multiple_of(quarter(j) * 32 + start, 16), n)]

    def relays(j):
        return (send(rows(xo, j, 0, 16), relay.at[0, j], a_s.at[0, j], a_r.at[0, j], ip, right),
                send(rows(xo, j, 16, 16), relay.at[1, j], a_s.at[1, j], a_r.at[1, j], ip, left))

    def fulls(j):
        return (send(rows(xp, j, 0, 32), in_got(x, j, 0, 32), a_s.at[2, j], a_r.at[2, j], ip, right),
                send(rows(xm, j, 0, 32), in_got(x, j, 0, 32), a_s.at[3, j], a_r.at[3, j], ip, left))

    def onward(j):
        return (send(relay.at[0, j], in_got(xm, j, 0, 16), a_s.at[4, j], a_r.at[4, j], ip, right),
                send(relay.at[1, j], in_got(xp, j, 16, 16), a_s.at[5, j], a_r.at[5, j], ip, left))

    def start_relays(j, carry):
        for copy in relays(j):
            copy.start()
        return carry

    def start_fulls(j, carry):
        for copy in fulls(j):
            copy.start()
        return carry

    def start_onward(j, carry):
        for copy, was in zip(onward(j), relays(j)):
            was.wait_recv()
            copy.start()
        return carry

    lax.fori_loop(0, 1, start_relays, 0)
    lax.fori_loop(0, 1, start_fulls, 0)
    lax.fori_loop(1, 4, start_relays, 0)
    swap_m = send(mask, mask2, v_s.at[0], v_r.at[0], partner, op)
    swap_v = send(v_hbm, vbuf.at[c], v_s.at[1], v_r.at[1], partner, op)
    swap_m.start()
    swap_v.start()

    def mask_half(half, m):
        for a in range(width // SUB_C):
            at = pl.ds(a * SUB_R, SUB_R)
            vbuf[half, at, :] = vbuf[half, at, :] * m[a:a + 1, :].astype(BF16)

    load_v.wait()
    mask_half(c, mask)
    lax.fori_loop(0, 1, start_onward, 0)

    def start_rest(j, carry):
        start_fulls(j, 0)
        return start_onward(j, carry)

    lax.fori_loop(1, 4, start_rest, 0)
    load_a.wait()

    def place(k):
        sub, rel = k % SUBS, (k // SUBS) % 2
        return quarter(k // (2 * SUBS)), rel, sub, c + rel * (1 - 2 * c)

    def select(j):
        for copy in (*fulls(j), *onward(j)):
            copy.wait_recv()
        for n in range(2 * SUBS):
            core = c + (n // SUBS) * (1 - 2 * c)
            for part_b in range(CH // 16):
                b = (n % SUBS) if SUBS == 2 else part_b
                holder = owner[b]
                at = pl.ds(pl.multiple_of(quarter(j) * 32 + core * 16, 16), 16)
                value = jnp.zeros((16, width), F32)
                for held in range(4):
                    value = value + got[held, at, :].astype(F32) * jnp.where(holder == zl * 4 + held, 1.0, 0.0)
                sel[j * 2 * SUBS + n, part_b * 16:(part_b + 1) * 16, :] = value.astype(BF16)

    far = HOP * jnp.maximum(zl, 7 - zl)
    near = HOP * jnp.minimum(zl, 7 - zl)

    def line_r_copy(k):
        return send(rout.at[k], rin.at[k], line_s.at[0, k], line_r.at[0, k], ip, op + 4)

    def line_l_copy(k):
        return send(lout.at[k], lin.at[k], line_s.at[1, k], line_r.at[1, k], ip, op - 4)

    def in_t(k, src_x):
        q, _, sub, _ = place(k)
        return q, pl.ds(pl.multiple_of(src_x * 32 + sub * 16, 16), CH)

    def ag_copies(k):
        q, at = in_t(k, x)
        core = place(k)[3]
        dst = t.at[c, q, at]
        to = ip - c + core
        return (send(fin.at[k], dst, ag_s.at[0, k], ag_r.at[0, k], to, right),
                send(fin.at[k], dst, ag_s.at[1, k], ag_r.at[1, k], to, left))

    def far_copy(k):
        q, at = in_t(k, x)
        to = ip - c + place(k)[3]
        return send(fin.at[k], t.at[c, q, at], ag_s.at[2, k], ag_r.at[2, k], to, across)

    def to_partner(k):
        q, at = in_t(k, x)
        return send(fin.at[k], t.at[c, q, at], ag_s.at[3, k], ag_r.at[3, k], partner, op)

    def by_kind(k, even, odd):
        rel = (k // SUBS) % 2

        @pl.when(rel == 0)
        def _():
            even()

        @pl.when(rel == 1)
        def _():
            odd()

    spare = jnp.where(near >= 2 * HOP, 0, near + NCH + 1)

    def line(step, carry):
        @pl.when(step == spare)
        def _():
            swap_m.wait_recv()
            swap_v.wait_recv()
            mask_half(other, mask2)

        kq = step - near

        @pl.when(jnp.logical_and(jnp.logical_and(kq >= 0, kq < NCH), kq % (2 * SUBS) == 0))
        def _():
            select(kq // (2 * SUBS))

        kr = step - HOP * zl

        @pl.when(jnp.logical_and(kr >= 0, kr < NCH))
        def _():
            @pl.when(zl > 0)
            def _():
                line_r_copy(kr).wait_recv()

            @pl.when(zl < 7)
            def _():
                rout[kr] = sel[kr] + rin[kr]
                line_r_copy(kr).start()

        kl = step - HOP * (7 - zl)

        @pl.when(jnp.logical_and(kl >= 0, kl < NCH))
        def _():
            @pl.when(zl < 7)
            def _():
                line_l_copy(kl).wait_recv()

            @pl.when(zl > 0)
            def _():
                lout[kl] = sel[kl] + lin[kl]
                line_l_copy(kl).start()

        kf = step - far

        @pl.when(jnp.logical_and(kf >= 0, kf < NCH))
        def _():
            value = sel[kf] + rin[kf] + lin[kf]
            fin[kf] = value

            def keep():
                q, at = in_t(kf, x)
                t[c, q, at, :] = value

            by_kind(kf, keep, lambda: to_partner(kf).start())
            for copy in ag_copies(kf):
                copy.start()
            far_copy(kf).start()

        return carry

    lax.fori_loop(0, far + NCH, line, 0)

    def arrived(k, carry):
        for copy in (*ag_copies(k), far_copy(k)):
            copy.wait_recv()
        by_kind(k, lambda: None, lambda: to_partner(k).wait_recv())
        return carry

    def zq(j):
        return (zh + (2, 1, 3, 0)[j]) % 4

    def product(j):
        lax.fori_loop(2 * SUBS * j, 2 * SUBS * (j + 1), arrived, 0)
        q = zq(j)

        def columns(n, carry):
            at = pl.ds(pl.multiple_of(n * 256, 256), 256)
            total = jnp.dot(t[0, q], vbuf[0, :, at], preferred_element_type=F32)
            total = total + jnp.dot(t[1, q], vbuf[1, :, at], preferred_element_type=F32)
            part[q, :, at] = total
            return carry

        lax.fori_loop(0, width // 256, columns, 0)

    FIRST = ((2, 0), (2, 1), (1, 1), (3, 0))
    SECOND = {4: (1, 0), 5: (3, 1)}
    LAST = ((3, 4), (2, 5))

    def y_copy(j, m):
        return send(ysend.at[j, m], yrecv.at[j, m], y_s.at[j, m], y_r.at[j, m], (y_up, y_down)[m % 2], op)

    def y_piece(j, d, h):
        return part[zq(j), pl.ds(pl.multiple_of(((y + d) % 4) * 32 + h * 16, 16), 16), :]

    def y_first(j):
        for m in range(4):
            quantize(ysend.at[j, m], y_piece(j, *FIRST[m]))
            y_copy(j, m).start()

    def y_second(j):
        for m in (4, 5):
            y_copy(j, m - 4).wait_recv()
            quantize(ysend.at[j, m], y_piece(j, *SECOND[m]) + restore(yrecv.at[j, m - 4], width))
            y_copy(j, m).start()

    def y_last(j):
        values = []
        for h in range(2):
            value = y_piece(j, 0, h)
            for m in LAST[h]:
                y_copy(j, m).wait_recv()
                value = value + restore(yrecv.at[j, m], width)
            values.append(value)
        return values

    def z_copy(m):
        return send(zsend.at[m], zrecv.at[m], z_s.at[m], z_r.at[m], (z_up, z_down)[m % 2], op)

    def z_send(m, value):
        quantize(zsend.at[m], value)
        z_copy(m).start()

    def z_join(value, m):
        z_copy(m).wait_recv()
        return value + restore(zrecv.at[m], width)

    product(0)
    y_first(0)
    product(1)
    y_first(1)
    y_second(0)
    product(2)
    y_first(2)
    y_second(1)
    opposite = y_last(0)
    z_send(0, opposite[0])
    z_send(1, opposite[1])
    product(3)
    y_first(3)
    y_second(2)
    above = y_last(1)
    z_send(2, above[1])
    y_second(3)
    below = y_last(2)
    z_send(3, below[0])
    part[zq(1), 0:16, :] = above[0]
    part[zq(2), 0:16, :] = below[1]
    own = y_last(3)
    mine[0:16, :] = own[0]
    mine[16:32, :] = own[1]
    z_send(4, z_join(part[zq(1), 0:16, :], 0))
    z_send(5, z_join(part[zq(2), 0:16, :], 1))
    for h in range(2):
        value = mine[h * 16:(h + 1) * 16, :]
        for m in LAST[h]:
            value = z_join(value, m)
        mine[h * 16:(h + 1) * 16, :] = value

    def d1_copy(n):
        at = pl.ds(pl.multiple_of(((zl + n) % 8) * 128, 128), 128)
        return send(mine.at[:, at], d1.at[zl], d1_s.at[n], d1_r.at[n], ip, along(n))

    for n in (4, 3, 5, 2, 6, 1, 7):
        d1_copy(n).start()
    d1[zl] = mine[:, pl.ds(pl.multiple_of(zl * 128, 128), 128)]
    for n in range(1, 8):
        d1_copy(n).wait_recv()
    packed = regroup([d1[:, r * 8:(r + 1) * 8, :].reshape(64, 128) for r in range(4)])
    for i in range(4):
        d2s[i] = packed[i]

    def d2_copy(n, to):
        return send(d2s.at[(x + n) % 4], d2r.at[x], d2_sem.at[n], d2_rem.at[n], ip, to)

    d2_copies = [d2_copy(2, across), d2_copy(1, right), d2_copy(3, left)]
    for copy in d2_copies:
        copy.start()
    d2r[x] = d2s[x]
    row = lax.broadcasted_iota(jnp.int32, (128, 128), 0)
    column = lax.broadcasted_iota(jnp.int32, (8, 128), 1)
    target = jnp.zeros((8, 128), jnp.int32)
    for g in range(GRP):
        target = jnp.where(column % GRP == g, swap[g] + (column // GRP) * GRP, target)
    pick = jnp.where(row == target[0:1, :], 1.0, 0.0).astype(BF16)
    for copy in d2_copies:
        copy.wait_recv()
    faced = regroup([d2r[i] for i in range(4)])
    for r in range(4):
        rest = faced[r]
        moved = jnp.zeros((64, 128), F32)
        for _ in range(3):
            piece = rest.astype(BF16)
            rest = rest - piece.astype(F32)
            moved = moved + jnp.dot(piece, pick, preferred_element_type=F32)
        for n in range(8):
            out[r // 2, (r % 2) * 8:(r % 2) * 8 + 8, n * 128:(n + 1) * 128] = (
                mine[r * 8:(r + 1) * 8, n * 128:(n + 1) * 128] + moved[n * 8:(n + 1) * 8, :])

    for copy in (swap_m, swap_v, *d2_copies):
        copy.wait_send()
    for n in range(1, 8):
        d1_copy(n).wait_send()
    for m in range(6):
        z_copy(m).wait_send()

    def drained_quarter(j, carry):
        for copy in (*relays(j), *fulls(j), *onward(j)):
            copy.wait_send()
        for m in range(6):
            y_copy(j, m).wait_send()
        return carry

    lax.fori_loop(0, 4, drained_quarter, 0)

    def drained(k, carry):
        @pl.when(zl < 7)
        def _():
            line_r_copy(k).wait_send()

        @pl.when(zl > 0)
        def _():
            line_l_copy(k).wait_send()

        for copy in (*ag_copies(k), far_copy(k)):
            copy.wait_send()
        by_kind(k, lambda: None, lambda: to_partner(k).wait_send())
        return carry

    lax.fori_loop(0, NCH, drained, 0)


def contract(owner, live, swap, integrals, amplitudes):
    any_spec = pl.BlockSpec(memory_space=pl.ANY)
    vmem = pl.BlockSpec(memory_space=pltpu.VMEM)
    dma = pltpu.SemaphoreType.DMA
    return pl.pallas_call(
        kernel,
        out_shape=jax.ShapeDtypeStruct((NB, 16, 1024), F32),
        in_specs=[pl.BlockSpec(memory_space=pltpu.SMEM)] * 3 + [any_spec, any_spec],
        out_specs=vmem,
        scratch_shapes=[
            pltpu.VMEM((8, 1024), F32),
            pltpu.VMEM((4, 128, 1024), BF16),
            pltpu.VMEM((2, 4, 16, 1024), BF16),
            pltpu.VMEM((2, 1024, 1024), BF16),
            pltpu.VMEM((8, 1024), F32),
            *[pltpu.VMEM((NCH, CH, 1024), BF16)] * 6,
            pltpu.VMEM((2, 4, 128, 1024), BF16),
            pltpu.VMEM((4, 128, 1024), F32),
            *[pltpu.VMEM((4, 6, 16, 1152), jnp.int16)] * 2,
            *[pltpu.VMEM((6, 16, 1152), jnp.int16)] * 2,
            pltpu.VMEM((32, 1024), F32),
            pltpu.VMEM((8, 32, 128), F32),
            *[pltpu.VMEM((4, 64, 128), F32)] * 2,
            dma((6, 4)), dma((6, 4)), dma((2,)), dma((2,)), dma((2,)),
            dma((2, NCH)), dma((2, NCH)), dma((4, NCH)), dma((4, NCH)),
            dma((4, 6)), dma((4, 6)), dma((6,)), dma((6,)),
            dma((8,)), dma((8,)), dma((4,)), dma((4,)),
        ],
        compiler_params=pltpu.CompilerParams(collective_id=0, has_side_effects=True,
                                             vmem_limit_bytes=VMEM_LIMIT),
    )(owner, live, swap, integrals, amplitudes)


def on_device(integrals, amplitudes, tile_live, batch_owner, occ_energy, vir_energy, swap_within):
    both = contract(batch_owner, tile_live, swap_within, integrals, amplitudes)
    return both / (vir_energy[None, None, :] - occ_energy[:, :, None])


def solution(mesh):
    return jax.shard_map(
        on_device,
        mesh=mesh,
        in_specs=(
            P("inpair", "outpair"),
            P("outpair", None, "inpair"),
            P("inpair", "outpair"),
            P(),
            P(None, "inpair"),
            P("outpair"),
            P(),
        ),
        out_specs=P(None, "inpair", "outpair"),
        check_vma=False,
    )
```
